512 devices in a mesh: leaf: 16 (over z), front: 32 (over y, x, core).
Axes of the slice: x: 4, y: 4, z: 16, core: 2. Of those that a mesh axis runs over, the one named last changes fastest.
Arguments:
- stacked: float32 [32, 16384, 896], P('front', 'leaf'), may hold values from -1.171875 to 1.171875, as said below
- row_owner: int32 [32, 640, 1], P('front', 'leaf'), may hold values from 0 to 31; in each aligned block of 40 rows (0 to 39, 40 to 79, ..., all dimensions but the last counted through in order) at most 3 rows name the same one
- dest_local: int32 [32, 640], P('front', 'leaf'), may hold values from 0 to 63
Outputs:
- pivot_rows: float32 [32, 256, 896], P('front', 'leaf')
- assembled: float32 [32, 1024, 640], P('front', 'leaf')
The draws below stay inside these ranges and needn't reach their ends.
Inputs may be any that keep to these rules, and one draw needn't show every extreme that they name: `stacked`: entries of a front's rows carry a scale of their row and one of their column. `row_owner`: among the 40 contribution rows of a front on one leaf index, no owner is named by more than 3 of them.
All inputs are finite; a program needn't handle non-finite values.
Results may differ from the reference program's by a relative error of at most 0.000076.
Values sent between devices are 32-bit elements; how exact they have to be, the bound alone decides.
No kernel may reach another device: no remote copies, remote signals or barrier semaphores. Data moves between devices by JAX's collectives and lax.ppermute only.
A program may use at most 64 MiB of HBM per device.

```python
import math
import jax
import jax.numpy as jnp
import numpy as np
from jax import lax

PIV = 256
PR_DEV = 64
COLS = 896
CB = 640
CB_DEV = 40
CAP = 3
FRONT_ROWS = 16384
N_LEAF = 16
N_FRONT = 32


def draw_stacked(key, part):
    keys = jax.random.split(jax.random.fold_in(key, 11), 3)
    shape = (N_FRONT, FRONT_ROWS, COLS)
    base = jnp.clip(jax.random.normal(keys[0], shape, jnp.float32), -6.0, 6.0)
    row_scale = jnp.exp(jax.random.uniform(keys[1], (N_FRONT, FRONT_ROWS, 1), jnp.float32, 0.0, math.log(10.0)))
    col_scale = jnp.exp(jax.random.uniform(keys[2], (N_FRONT, 1, COLS), jnp.float32, 0.0, math.log(10.0)))
    return base * row_scale * col_scale * (0.25 / math.sqrt(FRONT_ROWS))


def plant(values, key, least, largest):
    shape = values.shape
    spot = [jax.random.randint(jax.random.fold_in(key, axis), (), 0, shape[axis]) for axis in range(len(shape))]
    values = values.at[tuple(spot)].set(least)
    longest = shape.index(max(shape))
    spot[longest] = (spot[longest] + 1) % shape[longest]
    return values.at[tuple(spot)].set(largest)


def shared_out(own_key, own, number, rows, count, top, limit, lean):
    order = jax.random.permutation(own_key, count)
    crowded, common = shares(count, rows * top, limit, lean, True), shares(count, rows * top, limit, lean, False)
    places = jnp.arange(count)

    def named(lengths, offset_by):
        used = int((lengths > 0).sum())
        fixed = max(1, used // 4)
        shifted = fixed + (places - fixed + offset_by * (used - fixed)) % max(1, count - fixed)
        return jnp.zeros((count,), jnp.int32).at[order[jnp.where(places < fixed, places, shifted)]].set(jnp.asarray(lengths, jnp.int32))

    lengths = jnp.where(number % 4 == 0, named(crowded, number // 4), named(common, number - number // 4 - 1))
    mixed = jax.random.permutation(jax.random.fold_in(own, 3), count)
    giver, receiver = mixed[0:count // 2 * 2:2], mixed[1:count // 2 * 2:2]
    margin = jnp.minimum(lengths[giver] - 1, limit - lengths[receiver]) // 2
    margin = jnp.where((giver == order[0]) | (receiver == order[0]) | (lengths[receiver] == 0), 0, jnp.maximum(margin, 0))
    shifted = jax.random.randint(jax.random.fold_in(own, 4), (count // 2,), 0, 1 << 20) % (margin + 1)
    lengths = lengths.at[giver].add(-shifted).at[receiver].add(shifted)
    members = jnp.searchsorted(jnp.cumsum(lengths), jnp.arange(rows * top), side="right").astype(jnp.int32)
    table = members.reshape(top, rows).T
    table = table[jax.random.permutation(jax.random.fold_in(own, 1), rows)]
    offset_by = jax.random.randint(jax.random.fold_in(own, 2), (rows, 1), 0, top)
    return jnp.take_along_axis(table, (jnp.arange(top)[None, :] + offset_by) % top, axis=1)


def shares(number_of, total, limit, slope, full):
    loads = [(1 << 20) // math.isqrt(standing ** slope) + 1 for standing in range(1, number_of + 1)]
    largest = limit if full else min(limit, max(-(-total // number_of), total * loads[0] // sum(loads)))
    least = 1 if total - largest >= number_of - 1 else 0
    counts, spare = [largest] + [least] * (number_of - 1), total - largest - least * (number_of - 1)
    while spare > 0:
        candidates = [i for i in range(1, number_of) if counts[i] < largest] or [i for i in range(1, number_of) if counts[i] < limit]
        pool, remaining = sum([loads[i] for i in candidates]), spare
        for i in candidates:
            more = min(limit - counts[i], max(1, remaining * loads[i] // pool), spare)
            counts[i] = counts[i] + more
            spare = spare - more
    return np.array(counts)


def setup_inputs(seed: int = 0) -> dict:
    splits = jax.random.split(jax.random.key(seed), 4)
    stacked = draw_stacked(jax.random.fold_in(splits[3], 71), 0)
    row_owner_keys = jax.random.split(jax.random.fold_in(splits[1], 1), N_FRONT * CB // CB_DEV)
    row_owner_turns = jax.random.permutation(jax.random.fold_in(splits[1], 3), N_FRONT * CB // CB_DEV)
    row_owner = jax.vmap(lambda own, number: shared_out(jax.random.fold_in(splits[1], 2), own, number, CB_DEV, N_FRONT, 1, CAP, 2))(row_owner_keys, row_owner_turns).reshape((N_FRONT, CB, 1))
    dest_local = plant(jax.random.randint(splits[2], (N_FRONT, CB), 0, PR_DEV), jax.random.fold_in(splits[2], 1), 0, PR_DEV - 1).astype(jnp.int32)
    return {"stacked": stacked, "row_owner": row_owner, "dest_local": dest_local}


highest = lax.Precision.HIGHEST

def front_factor(front_rows):
    gram_front = lax.dot_general(front_rows.astype(jnp.float32), front_rows.astype(jnp.float32), (((0,), (0,)), ((), ())), precision=highest, preferred_element_type=jnp.float32)
    return jnp.linalg.cholesky(gram_front).T

def reference(stacked, row_owner, dest_local):
    factors = lax.map(front_factor, stacked)
    pivots = factors[:, :PIV, :]
    contribution = factors[:, PIV:, PIV:]
    width = contribution.shape[2]
    leaf_of_row = (jnp.arange(width).astype(jnp.int32) // CB_DEV).astype(jnp.int32)
    target = row_owner[:, :, 0].astype(jnp.int32) * (N_LEAF * PR_DEV) + leaf_of_row[None, :] * PR_DEV + dest_local.astype(jnp.int32)
    flat_rows = contribution.reshape(-1, width)
    summed = jnp.zeros((N_FRONT * N_LEAF * PR_DEV, width), jnp.float32).at[target.reshape(-1)].add(flat_rows)
    return (pivots, summed.reshape(N_FRONT, N_LEAF * PR_DEV, width))
```

```python
import functools
import jax
import jax.numpy as jnp
from jax import lax
from jax.experimental import pallas as pl
from jax.experimental.pallas import tpu as pltpu
from jax.sharding import PartitionSpec as P

PIV = 256
PR_DEV = 64
COLS = 896
CB = 640
CB_DEV = 40
CAP = 3
T = 128
NT = COLS // T
SUB = 8
NLEAF = 16
NFRONT = 32
PACKED = NT * (NT + 1) // 2 * T
SHARD = PACKED // NLEAF
PAD_SHARD = SHARD + 1
UNIT = 16
F32 = jnp.float32
BF16 = jnp.bfloat16
HIGHEST = lax.Precision.HIGHEST


def tile_index(i, j):
    return i * NT - i * (i - 1) // 2 + (j - i)


def halves(x):
    high = x.astype(BF16)
    return high, (x - high.astype(F32)).astype(BF16)


def dot_t(a, b):
    return lax.dot_general(a, b, (((0,), (0,)), ((), ())), preferred_element_type=F32)


def dot3_t(a, b):
    return dot_t(a[0], b[0]) + (dot_t(a[0], b[1]) + dot_t(a[1], b[0]))


def dot3(a, b):
    mm = functools.partial(jnp.dot, preferred_element_type=F32)
    return mm(a[0], b[0]) + (mm(a[0], b[1]) + mm(a[1], b[0]))


def gram_kernel(x_ref, out_ref, acc_ref):
    step = pl.program_id(0)

    @pl.when(step == 0)
    def _():
        acc_ref[...] = jnp.zeros_like(acc_ref)

    high, low = halves(x_ref[0])
    for start in range(0, COLS, 2 * T):
        stop = min(start + 2 * T, COLS)
        a = (high[:, :stop], low[:, :stop])
        b = (high[:, start:stop], low[:, start:stop])
        block = dot3_t(a, b)
        for j in range(start // T, stop // T):
            for i in range(j + 1):
                row = tile_index(i, j) * T
                acc_ref[row : row + T, :] += block[i * T : (i + 1) * T, j * T - start : (j + 1) * T - start]

    @pl.when(step == pl.num_programs(0) - 1)
    def _():
        for z in range(NLEAF):
            out_ref[z * PAD_SHARD : z * PAD_SHARD + SHARD, :] = acc_ref[z * SHARD : (z + 1) * SHARD, :]
            out_ref[z * PAD_SHARD + SHARD : (z + 1) * PAD_SHARD, :] = jnp.zeros((PAD_SHARD - SHARD, T), F32)


def local_gram(stacked):
    rows = stacked.shape[1]
    chunk = 256
    return pl.pallas_call(
        gram_kernel,
        out_shape=jax.ShapeDtypeStruct((NLEAF * PAD_SHARD, T), F32),
        grid=(rows // chunk,),
        in_specs=[pl.BlockSpec((1, chunk, COLS), lambda k: (0, k, 0))],
        out_specs=pl.BlockSpec((NLEAF * PAD_SHARD, T), lambda k: (0, 0)),
        scratch_shapes=[pltpu.VMEM((PACKED, T), F32)],
        name="local_gram",
    )(stacked)


def lanes_of(x, lane):
    return jnp.broadcast_to(x[:, lane : lane + 1], (SUB, T))


def row_of(x, row):
    return jnp.broadcast_to(x[row : row + 1, :], (SUB, T))


def diagonal_factor(d_ref, inv_ref):
    lane = lax.broadcasted_iota(jnp.int32, (SUB, T), 1)
    sub = lax.broadcasted_iota(jnp.int32, (SUB, T), 0)
    nb = T // SUB
    rows = [d_ref[SUB * i : SUB * (i + 1), :] for i in range(nb)]
    unit = [(lane == sub + SUB * i).astype(F32) for i in range(nb)]
    for b in range(nb):
        c0 = SUB * b
        columns = [lanes_of(rows[b], c0 + k) for k in range(SUB)]
        s = [[None] * SUB for _ in range(SUB)]
        for i in range(SUB):
            for k in range(i + 1):
                s[i][k] = s[k][i] = row_of(columns[k], i)
        r = [row_of(rows[b], k) for k in range(SUB)]
        e = [row_of(unit[b], k) for k in range(SUB)]
        for k in range(SUB):
            root = lax.rsqrt(s[k][k])
            inverse = root * root
            at = c0 + k
            u = jnp.where(lane >= c0 + k, r[k] * root, 0.0)
            d_ref[at : at + 1, :] = u[0:1, :]
            inv_ref[at : at + 1, :] = (e[k] * root)[0:1, :]
            t = [s[k][j] * inverse if j > k else None for j in range(SUB)]
            pr = r[k] * inverse
            pe = e[k] * inverse
            for i in range(SUB):
                if i == k:
                    continue
                f = s[i][k]
                for j in range(k + 1, SUB):
                    if i < k or j >= i:
                        s[i][j] = s[i][j] - f * t[j]
                        if i > k:
                            s[j][i] = s[i][j]
                r[i] = r[i] - f * pr
                e[i] = e[i] - f * pe
            for j in range(k + 1, SUB):
                s[k][j] = t[j]
            r[k] = pr
            e[k] = pe
        for i in range(b + 1, nb):
            columns = [lanes_of(rows[i], c0 + k) for k in range(SUB)]
            acc_r = columns[0] * r[0]
            acc_e = columns[0] * e[0]
            for k in range(1, SUB):
                acc_r = acc_r + columns[k] * r[k]
                acc_e = acc_e + columns[k] * e[k]
            rows[i] = rows[i] - acc_r
            unit[i] = unit[i] - acc_e


def update_after(p, s_ref, d_ref, inv_ref):
    base = p * T
    after = base + T
    s_ref[base:after, base:after] = d_ref[...]
    if after == COLS:
        return
    panel = dot3(halves(inv_ref[...]), halves(s_ref[base:after, after:]))
    s_ref[base:after, after:] = panel
    split = halves(panel)
    for i in range(p + 1, NT):
        lo = i * T - after
        left = tuple(v[:, lo : lo + T] for v in split)
        right = tuple(v[:, lo:] for v in split)
        block = s_ref[i * T : (i + 1) * T, i * T :] - dot3_t(left, right)
        s_ref[i * T : (i + 1) * T, i * T :] = block
        if i == p + 1:
            d_ref[...] = block[:, :T]


def factor_kernel(g1_ref, g2_ref, owner_row_ref, owner_ref, dest_ref, leaf_ref, piv_ref, pay_ref, s_ref, d_ref, inv_ref):
    half = SHARD // 2
    per = half // UNIT
    for i in range(NT):
        for j in range(NT):
            if j < i:
                s_ref[i * T : (i + 1) * T, j * T : (j + 1) * T] = jnp.zeros((T, T), F32)
                continue
            for u in range(T // UNIT):
                g = tile_index(i, j) * (T // UNIT) + u
                z, rest = divmod(g, 2 * per)
                src = g1_ref if rest < per else g2_ref
                row = (z * per + rest % per) * UNIT
                s_ref[i * T + u * UNIT : i * T + (u + 1) * UNIT, j * T : (j + 1) * T] = src[row : row + UNIT, :]
    d_ref[...] = s_ref[:T, :T]

    def panel_step(p, _):
        diagonal_factor(d_ref, inv_ref)
        for q in range(NT):
            pl.when(p == q)(functools.partial(update_after, q, s_ref, d_ref, inv_ref))
        return 0

    lax.fori_loop(0, NT, panel_step, 0)
    leaf = leaf_ref[0]
    piv_ref[0] = s_ref[pl.ds(pl.multiple_of(leaf * (PIV // NLEAF), 8), PIV // NLEAF), :]
    block = s_ref[pl.ds(pl.multiple_of(PIV + leaf * CB_DEV, 8), CB_DEV), PIV:]
    owner = owner_ref[...]
    same = owner == owner_row_ref[...]
    earlier = lax.broadcasted_iota(jnp.int32, (CB_DEV, CB_DEV), 1) < lax.broadcasted_iota(jnp.int32, (CB_DEV, CB_DEV), 0)
    slot = jnp.sum(jnp.where(same & earlier, 1.0, 0.0), axis=1, keepdims=True).astype(jnp.int32)
    place = slot * NFRONT + owner
    pick = (place == lax.broadcasted_iota(jnp.int32, (CB_DEV, CAP * NFRONT), 1)).astype(F32)
    marks = jnp.broadcast_to((dest_ref[...] + 1).astype(F32), (CB_DEV, T))
    send = lax.dot_general(
        pick, jnp.concatenate([block, marks], axis=1), (((0,), (0,)), ((), ())), precision=HIGHEST, preferred_element_type=F32
    )
    lane = lax.broadcasted_iota(jnp.int32, (NFRONT, T), 1)
    meta = jnp.zeros((NFRONT, T), F32)
    for k in range(CAP):
        part = send[k * NFRONT : (k + 1) * NFRONT, :]
        for t in range(CB // T):
            pay_ref[pl.ds(k * (CB // T) + t, NFRONT, stride=16), :] = part[:, t * T : (t + 1) * T]
        meta = jnp.where(lane == k, part[:, CB:], meta)
    pay_ref[pl.ds(15, NFRONT, stride=16), :] = meta


def factor(g1, g2, owner_row, owner, dest, leaf):
    vmem = pl.BlockSpec(memory_space=pltpu.VMEM)
    return pl.pallas_call(
        factor_kernel,
        out_shape=(
            jax.ShapeDtypeStruct((1, PIV // NLEAF, COLS), F32),
            jax.ShapeDtypeStruct((NFRONT * 16, T), F32),
        ),
        in_specs=[vmem] * 5 + [pl.BlockSpec(memory_space=pltpu.SMEM)],
        out_specs=(vmem, vmem),
        scratch_shapes=[pltpu.VMEM((COLS, COLS), F32), pltpu.VMEM((T, T), F32), pltpu.VMEM((T, T), F32)],
        name="factor",
    )(g1, g2, owner_row, owner, dest, leaf)


def assemble_kernel(pay_ref, out_ref):
    meta = pay_ref[pl.ds(15, NFRONT, stride=16), :]
    target = lax.broadcasted_iota(jnp.int32, (NFRONT, PR_DEV), 1).astype(F32) + 1.0
    total = jnp.zeros((PR_DEV, CB), F32)
    for k in range(CAP):
        hits = (meta[:, k : k + 1] == target).astype(F32)
        rows = jnp.concatenate(
            [pay_ref[pl.ds(k * (CB // T) + t, NFRONT, stride=16), :] for t in range(CB // T)], axis=1
        )
        total = total + lax.dot_general(
            hits, rows, (((0,), (0,)), ((), ())), precision=HIGHEST, preferred_element_type=F32
        )
    out_ref[0] = total


def assemble(pay):
    vmem = pl.BlockSpec(memory_space=pltpu.VMEM)
    return pl.pallas_call(
        assemble_kernel,
        out_shape=jax.ShapeDtypeStruct((1, PR_DEV, CB), F32),
        in_specs=[vmem],
        out_specs=vmem,
        name="assemble",
    )(pay)


def shards(stacked, row_owner, dest_local):
    gram = local_gram(stacked)
    piece = lax.optimization_barrier(lax.psum_scatter(gram, "leaf", scatter_dimension=0, tiled=True))
    half = SHARD // 2
    g1 = lax.all_gather(piece[:half], "leaf", axis=0, tiled=True)
    g2 = lax.all_gather(piece[half:SHARD], "leaf", axis=0, tiled=True)
    owner = row_owner[0]
    dest = dest_local.reshape(CB_DEV, 1)
    leaf = lax.axis_index("leaf").astype(jnp.int32).reshape(1)
    piv, pay = factor(g1, g2, owner.reshape(1, CB_DEV), owner, dest, leaf)
    got = lax.all_to_all(pay, "front", 0, 0, tiled=True)
    return piv, assemble(got)


def solution(mesh):
    return jax.shard_map(
        shards,
        mesh=mesh,
        in_specs=(P("front", "leaf", None), P("front", "leaf", None), P("front", "leaf")),
        out_specs=(P("front", "leaf", None), P("front", "leaf", None)),
        check_vma=False,
    )
```

```python
import functools
import jax
import jax.numpy as jnp
from jax import lax
from jax.experimental import pallas as pl
from jax.experimental.pallas import tpu as pltpu
from jax.sharding import PartitionSpec as P

PIV = 256
PR_DEV = 64
COLS = 896
CB = 640
CB_DEV = 40
CAP = 3
T = 128
NT = COLS // T
SUB = 8
NLEAF = 16
NFRONT = 32
PACKED = NT * (NT + 1) // 2 * T
SHARD = PACKED // NLEAF
PAD_SHARD = SHARD + 1
UNIT = 16
F32 = jnp.float32
BF16 = jnp.bfloat16
HIGHEST = lax.Precision.HIGHEST


def tile_index(i, j):
    return i * NT - i * (i - 1) // 2 + (j - i)


def halves(x):
    high = x.astype(BF16)
    return high, (x - high.astype(F32)).astype(BF16)


def dot_t(a, b):
    return lax.dot_general(a, b, (((0,), (0,)), ((), ())), preferred_element_type=F32)


def dot3_t(a, b):
    return dot_t(a[0], b[0]) + (dot_t(a[0], b[1]) + dot_t(a[1], b[0]))


def dot3(a, b):
    mm = functools.partial(jnp.dot, preferred_element_type=F32)
    return mm(a[0], b[0]) + (mm(a[0], b[1]) + mm(a[1], b[0]))


def gram_kernel(x_ref, out_ref, acc_ref):
    step = pl.program_id(0)

    @pl.when(step == 0)
    def _():
        acc_ref[...] = jnp.zeros_like(acc_ref)

    high, low = halves(x_ref[0])
    for start in range(0, COLS, 2 * T):
        stop = min(start + 2 * T, COLS)
        a = (high[:, :stop], low[:, :stop])
        b = (high[:, start:stop], low[:, start:stop])
        block = dot3_t(a, b)
        for j in range(start // T, stop // T):
            for i in range(j + 1):
                row = tile_index(i, j) * T
                acc_ref[row : row + T, :] += block[i * T : (i + 1) * T, j * T - start : (j + 1) * T - start]

    @pl.when(step == pl.num_programs(0) - 1)
    def _():
        for z in range(NLEAF):
            out_ref[z * PAD_SHARD : z * PAD_SHARD + SHARD, :] = acc_ref[z * SHARD : (z + 1) * SHARD, :]
            out_ref[z * PAD_SHARD + SHARD : (z + 1) * PAD_SHARD, :] = jnp.zeros((PAD_SHARD - SHARD, T), F32)


def local_gram(stacked):
    rows = stacked.shape[1]
    chunk = 256
    return pl.pallas_call(
        gram_kernel,
        out_shape=jax.ShapeDtypeStruct((NLEAF * PAD_SHARD, T), F32),
        grid=(rows // chunk,),
        in_specs=[pl.BlockSpec((1, chunk, COLS), lambda k: (0, k, 0))],
        out_specs=pl.BlockSpec((NLEAF * PAD_SHARD, T), lambda k: (0, 0)),
        scratch_shapes=[pltpu.VMEM((PACKED, T), F32)],
        name="local_gram",
        compiler_params=pltpu.CompilerParams(vmem_limit_bytes=61 << 20),
    )(stacked)


def lanes_of(x, lane):
    return jnp.take_along_axis(x, jnp.full((SUB, T), lane, jnp.int32), axis=1)


def row_of(x, row):
    return jnp.broadcast_to(x[row : row + 1, :], (SUB, T))


def diagonal_factor(d_ref, inv_ref):
    lane = lax.broadcasted_iota(jnp.int32, (SUB, T), 1)
    sub = lax.broadcasted_iota(jnp.int32, (SUB, T), 0)
    is_row = [sub == k for k in range(SUB)]
    nb = T // SUB
    rows = [d_ref[SUB * i : SUB * (i + 1), :] for i in range(nb)]
    for b in range(nb):
        c0 = SUB * b
        inside = (lane >= c0) & (lane < c0 + SUB)
        col = [lanes_of(rows[b], c0 + k) for k in range(SUB)]
        work = jnp.where(inside, (lane == sub + c0).astype(F32), rows[b])
        done = jnp.zeros((SUB, T), F32)
        for k in range(SUB):
            root = lax.rsqrt(row_of(col[k], k))
            inverse = root * root
            ahead = [row_of(col[j], k) if j > k else None for j in range(SUB)]
            for j in range(k + 1, SUB):
                prod = col[k] * ahead[j]
                col[j] = jnp.where(is_row[k], ahead[j] * inverse, col[j] - prod * inverse)
            rk = row_of(work, k)
            done = jnp.where(is_row[k], rk * root, done)
            pk = rk * inverse
            work = jnp.where(is_row[k], pk, work - col[k] * pk)
        inv_ref[c0 : c0 + SUB, :] = jnp.where(lane < c0 + SUB, done, 0.0)
        if b + 1 < nb:
            solved = [row_of(work, k) for k in range(SUB)]
        for i in range(b + 1, nb):
            terms = [lanes_of(rows[i], c0 + k) * solved[k] for k in range(SUB)]
            while len(terms) > 1:
                terms = [terms[q] + terms[q + 1] for q in range(0, len(terms), 2)]
            rows[i] = jnp.where(inside, 0.0, rows[i]) - terms[0]


def update_after(p, s_ref, d_ref, inv_ref):
    base = p * T
    after = base + T
    panel = dot3(halves(inv_ref[...]), halves(s_ref[base:after, base:]))
    upper = lax.broadcasted_iota(jnp.int32, (T, T), 1) >= lax.broadcasted_iota(jnp.int32, (T, T), 0)
    s_ref[base:after, base:after] = jnp.where(upper, panel[:, :T], 0.0)
    if after == COLS:
        return
    panel = panel[:, T:]
    s_ref[base:after, after:] = panel
    split = halves(panel)
    for i in range(p + 1, NT):
        lo = i * T - after
        left = tuple(v[:, lo : lo + T] for v in split)
        right = tuple(v[:, lo:] for v in split)
        block = s_ref[i * T : (i + 1) * T, i * T :] - dot3_t(left, right)
        s_ref[i * T : (i + 1) * T, i * T :] = block
        if i == p + 1:
            d_ref[...] = block[:, :T]


def unpack(mine, parity, g_ref, low_ref, high_ref, s_ref):
    per = SHARD // UNIT
    for i in range(NT):
        for j in range(i, NT):
            for u in range(T // UNIT):
                z, rest = divmod(tile_index(i, j) * (T // UNIT) + u, per)
                if (z % 2 == parity) != mine:
                    continue
                row = (z // 2 * per + rest) * UNIT
                src = g_ref
                if not mine:
                    half = NLEAF // 4 * SHARD
                    src, row = (low_ref, row) if row < half else (high_ref, row - half)
                s_ref[i * T + u * UNIT : i * T + (u + 1) * UNIT, j * T : (j + 1) * T] = src[row : row + UNIT, :]


def factor_kernel(g_ref, low_ref, high_ref, owner_row_ref, owner_ref, dest_ref, leaf_ref, piv_ref, pay_ref, s_ref, d_ref, inv_ref):
    for i in range(NT):
        for j in range(i):
            s_ref[i * T : (i + 1) * T, j * T : (j + 1) * T] = jnp.zeros((T, T), F32)
    leaf = leaf_ref[0]
    for parity in range(2):

        @pl.when(lax.rem(leaf, 2) == parity)
        def _():
            for mine in (True, False):
                unpack(mine, parity, g_ref, low_ref, high_ref, s_ref)

    d_ref[...] = s_ref[:T, :T]

    def panel_step(p, _):
        diagonal_factor(d_ref, inv_ref)
        for q in range(NT):
            pl.when(p == q)(functools.partial(update_after, q, s_ref, d_ref, inv_ref))
        return 0

    lax.fori_loop(0, NT, panel_step, 0)
    piv_ref[0] = s_ref[pl.ds(pl.multiple_of(leaf * (PIV // NLEAF), 8), PIV // NLEAF), :]
    block = s_ref[pl.ds(pl.multiple_of(PIV + leaf * CB_DEV, 8), CB_DEV), PIV:]
    owner = owner_ref[...]
    same = owner == owner_row_ref[...]
    earlier = lax.broadcasted_iota(jnp.int32, (CB_DEV, CB_DEV), 1) < lax.broadcasted_iota(jnp.int32, (CB_DEV, CB_DEV), 0)
    slot = jnp.sum(jnp.where(same & earlier, 1.0, 0.0), axis=1, keepdims=True).astype(jnp.int32)
    place = slot * NFRONT + owner
    pick = (place == lax.broadcasted_iota(jnp.int32, (CB_DEV, CAP * NFRONT), 1)).astype(F32)
    marks = jnp.broadcast_to((dest_ref[...] + 1).astype(F32), (CB_DEV, T))
    send = lax.dot_general(
        pick, jnp.concatenate([block, marks], axis=1), (((0,), (0,)), ((), ())), precision=HIGHEST, preferred_element_type=F32
    )
    lane = lax.broadcasted_iota(jnp.int32, (NFRONT, T), 1)
    meta = jnp.zeros((NFRONT, T), F32)
    for k in range(CAP):
        part = send[k * NFRONT : (k + 1) * NFRONT, :]
        for t in range(CB // T):
            pay_ref[pl.ds(k * (CB // T) + t, NFRONT, stride=16), :] = part[:, t * T : (t + 1) * T]
        meta = jnp.where(lane == k, part[:, CB:], meta)
    pay_ref[pl.ds(15, NFRONT, stride=16), :] = meta


def factor(g, low, high, owner_row, owner, dest, leaf):
    vmem = pl.BlockSpec(memory_space=pltpu.VMEM)
    return pl.pallas_call(
        factor_kernel,
        out_shape=(
            jax.ShapeDtypeStruct((1, PIV // NLEAF, COLS), F32),
            jax.ShapeDtypeStruct((NFRONT * 16, T), F32),
        ),
        in_specs=[vmem] * 6 + [pl.BlockSpec(memory_space=pltpu.SMEM)],
        out_specs=(vmem, vmem),
        scratch_shapes=[pltpu.VMEM((COLS, COLS), F32), pltpu.VMEM((T, T), F32), pltpu.VMEM((T, T), F32)],
        name="factor",
        compiler_params=pltpu.CompilerParams(vmem_limit_bytes=24 << 20),
    )(g, low, high, owner_row, owner, dest, leaf)


def assemble_kernel(pay_ref, out_ref):
    meta = pay_ref[pl.ds(15, NFRONT, stride=16), :]
    target = lax.broadcasted_iota(jnp.int32, (NFRONT, PR_DEV), 1).astype(F32) + 1.0
    total = jnp.zeros((PR_DEV, CB), F32)
    for k in range(CAP):
        hits = (meta[:, k : k + 1] == target).astype(F32)
        rows = jnp.concatenate(
            [pay_ref[pl.ds(k * (CB // T) + t, NFRONT, stride=16), :] for t in range(CB // T)], axis=1
        )
        total = total + lax.dot_general(
            hits, rows, (((0,), (0,)), ((), ())), precision=HIGHEST, preferred_element_type=F32
        )
    out_ref[0] = total


def assemble(pay):
    vmem = pl.BlockSpec(memory_space=pltpu.VMEM)
    return pl.pallas_call(
        assemble_kernel,
        out_shape=jax.ShapeDtypeStruct((1, PR_DEV, CB), F32),
        in_specs=[vmem],
        out_specs=vmem,
        name="assemble",
        compiler_params=pltpu.CompilerParams(vmem_limit_bytes=16 << 20),
    )(pay)


def shards(stacked, row_owner, dest_local):
    gram = local_gram(stacked)
    piece = lax.optimization_barrier(lax.psum_scatter(gram, "leaf", scatter_dimension=0, tiled=True))
    groups = [list(range(first, NLEAF, 2)) for first in range(2)]
    own = lax.all_gather(piece[:SHARD], "leaf", axis=0, tiled=True, axis_index_groups=groups)
    half = NLEAF // 4 * SHARD
    low = lax.ppermute(own[:half], "leaf", [(z, (z + 1) % NLEAF) for z in range(NLEAF)])
    high = lax.ppermute(own[half:], "leaf", [(z, (z - 1) % NLEAF) for z in range(NLEAF)])
    owner = row_owner[0]
    dest = dest_local.reshape(CB_DEV, 1)
    leaf = lax.axis_index("leaf").astype(jnp.int32).reshape(1)
    piv, pay = factor(own, low, high, owner.reshape(1, CB_DEV), owner, dest, leaf)
    got = lax.all_to_all(pay, "front", 0, 0, tiled=True)
    return piv, assemble(got)


def solution(mesh):
    return jax.shard_map(
        shards,
        mesh=mesh,
        in_specs=(P("front", "leaf", None), P("front", "leaf", None), P("front", "leaf")),
        out_specs=(P("front", "leaf", None), P("front", "leaf", None)),
        check_vma=False,
    )
```

```python
import functools
import jax
import jax.numpy as jnp
from jax import lax
from jax.experimental import pallas as pl
from jax.experimental.pallas import tpu as pltpu
from jax.sharding import PartitionSpec as P

PIV = 256
PR_DEV = 64
COLS = 896
CB = 640
CB_DEV = 40
CAP = 3
T = 128
NT = COLS // T
SUB = 8
NLEAF = 16
NFRONT = 32
PAIRS = ((0, 1), (2, 3), (4, 5))
LONE = NT - 1
TILES = NT * (NT + 1) // 2
FULL = (TILES - len(PAIRS)) * T
SHARD = 201
HALF = NLEAF // 4
F32 = jnp.float32
BF16 = jnp.bfloat16
HIGHEST = lax.Precision.HIGHEST


def tile_index(i, j):
    return i * NT - i * (i - 1) // 2 + (j - i)


def packed_tiles():
    order = [(i, j) for i in range(NT) for j in range(i + 1, NT)]
    return order + [(LONE, LONE)] + [(p, p) for p, _ in PAIRS]


def pieces(start, stop):
    while start < stop:
        chunk, rest = divmod(start, SHARD)
        size = min(stop - start, SHARD - rest)
        yield start, chunk, rest, size
        start += size


def square_iota(axis):
    return lax.broadcasted_iota(jnp.int32, (T, T), axis)


def halves(x):
    high = x.astype(BF16)
    return high, (x - high.astype(F32)).astype(BF16)


def dot_t(a, b):
    return lax.dot_general(a, b, (((0,), (0,)), ((), ())), preferred_element_type=F32)


def dot3_t(a, b):
    return dot_t(a[0], b[0]) + (dot_t(a[0], b[1]) + dot_t(a[1], b[0]))


def dot3(a, b):
    mm = functools.partial(jnp.dot, preferred_element_type=F32)
    return mm(a[0], b[0]) + (mm(a[0], b[1]) + mm(a[1], b[0]))


def gram_kernel(x_ref, out_ref, acc_ref):
    step = pl.program_id(0)

    @pl.when(step == 0)
    def _():
        acc_ref[...] = jnp.zeros_like(acc_ref)

    high, low = halves(x_ref[0])
    for start in range(0, COLS, 2 * T):
        stop = min(start + 2 * T, COLS)
        a = (high[:, :stop], low[:, :stop])
        b = (high[:, start:stop], low[:, start:stop])
        block = dot3_t(a, b)
        for j in range(start // T, stop // T):
            for i in range(j + 1):
                row = tile_index(i, j) * T
                acc_ref[row : row + T, :] += block[i * T : (i + 1) * T, j * T - start : (j + 1) * T - start]

    @pl.when(step == pl.num_programs(0) - 1)
    def _():
        def tile(i, j):
            row = tile_index(i, j) * T
            return acc_ref[row : row + T, :]

        row, col = square_iota(0), square_iota(1)
        partner = dict(PAIRS)
        for n, (i, j) in enumerate(packed_tiles()):
            value = tile(i, j)
            if i == j and i in partner:
                q = partner[i]
                other = tile(q, q)
                value = jnp.where(row <= col, value, other)
                at = FULL + PAIRS.index((i, q))
                out_ref[at : at + 1, :] = jnp.sum(jnp.where(row == col, other, 0.0), axis=0, keepdims=True)
            out_ref[n * T : (n + 1) * T, :] = value
        spare = FULL + len(PAIRS)
        out_ref[spare : NLEAF * SHARD, :] = jnp.zeros((NLEAF * SHARD - spare, T), F32)


def local_gram(stacked):
    rows = stacked.shape[1]
    chunk = 512
    return pl.pallas_call(
        gram_kernel,
        out_shape=jax.ShapeDtypeStruct((NLEAF * SHARD, T), F32),
        grid=(rows // chunk,),
        in_specs=[pl.BlockSpec((1, chunk, COLS), lambda k: (0, k, 0))],
        out_specs=pl.BlockSpec((NLEAF * SHARD, T), lambda k: (0, 0)),
        scratch_shapes=[pltpu.VMEM((TILES * T, T), F32)],
        name="local_gram",
        compiler_params=pltpu.CompilerParams(vmem_limit_bytes=61 << 20),
    )(stacked)


def lanes_of(x, lane):
    return jnp.take_along_axis(x, jnp.full((SUB, T), lane, jnp.int32), axis=1)


def row_of(x, row):
    return jnp.broadcast_to(x[row : row + 1, :], (SUB, T))


def diagonal_factor(d_ref, inv_ref):
    lane = lax.broadcasted_iota(jnp.int32, (SUB, T), 1)
    sub = lax.broadcasted_iota(jnp.int32, (SUB, T), 0)
    is_row = [sub == k for k in range(SUB)]
    nb = T // SUB
    rows = [d_ref[SUB * i : SUB * (i + 1), :] for i in range(nb)]
    for b in range(nb):
        c0 = SUB * b
        inside = (lane >= c0) & (lane < c0 + SUB)
        col = [lanes_of(rows[b], c0 + k) for k in range(SUB)]
        work = jnp.where(inside, (lane == sub + c0).astype(F32), rows[b])
        done = jnp.zeros((SUB, T), F32)
        pivot = row_of(col[0], 0)
        for k in range(SUB):
            root = lax.rsqrt(pivot)
            inverse = root * root
            ahead = [row_of(col[j], k) if j > k else None for j in range(SUB)]
            if k + 1 < SUB:
                pivot = row_of(col[k + 1], k + 1) - (ahead[k + 1] * ahead[k + 1]) * inverse
            for j in range(k + 1, SUB):
                prod = col[k] * ahead[j]
                col[j] = jnp.where(is_row[k], ahead[j] * inverse, col[j] - prod * inverse)
            rk = row_of(work, k)
            done = jnp.where(is_row[k], rk * root, done)
            pk = rk * inverse
            work = jnp.where(is_row[k], pk, work - col[k] * pk)
        inv_ref[c0 : c0 + SUB, :] = jnp.where(lane < c0 + SUB, done, 0.0)
        if b + 1 < nb:
            solved = [row_of(work, k) for k in range(SUB)]
        for i in range(b + 1, nb):
            terms = [lanes_of(rows[i], c0 + k) * solved[k] for k in range(SUB)]
            while len(terms) > 1:
                terms = [terms[q] + terms[q + 1] for q in range(0, len(terms), 2)]
            rows[i] = jnp.where(inside, 0.0, rows[i]) - terms[0]


def update_after(p, s_ref, d_ref, inv_ref):
    base = p * T
    after = base + T
    panel = dot3(halves(inv_ref[...]), halves(s_ref[base:after, base:]))
    upper = lax.broadcasted_iota(jnp.int32, (T, T), 1) >= lax.broadcasted_iota(jnp.int32, (T, T), 0)
    s_ref[base:after, base:after] = jnp.where(upper, panel[:, :T], 0.0)
    if after == COLS:
        return
    panel = panel[:, T:]
    s_ref[base:after, after:] = panel
    split = halves(panel)
    for i in range(p + 1, NT):
        lo = i * T - after
        left = tuple(v[:, lo : lo + T] for v in split)
        right = tuple(v[:, lo:] for v in split)
        block = s_ref[i * T : (i + 1) * T, i * T :] - dot3_t(left, right)
        s_ref[i * T : (i + 1) * T, i * T :] = block
        if i == p + 1:
            d_ref[...] = block[:, :T]


def unpack(parity, g_ref, low_ref, high_ref, s_ref, diag_ref):
    def move(dst, row, col, start, stop):
        for first, chunk, rest, size in pieces(start, stop):
            member = chunk // 2
            src = g_ref
            if chunk % 2 != parity:
                src, member = (low_ref, member) if member < HALF else (high_ref, member - HALF)
            to = row + first - start
            dst[to : to + size, col : col + T] = src[member, rest : rest + size, :]

    for n, (i, j) in enumerate(packed_tiles()):
        move(s_ref, i * T, j * T, n * T, (n + 1) * T)
    move(diag_ref, 0, 0, FULL, FULL + len(PAIRS))


def split_pairs(s_ref, diag_ref):
    row, col = square_iota(0), square_iota(1)
    for n, (p, q) in enumerate(PAIRS):
        both = s_ref[p * T : (p + 1) * T, p * T : (p + 1) * T]
        turned = jnp.transpose(both)
        s_ref[p * T : (p + 1) * T, p * T : (p + 1) * T] = jnp.where(row <= col, both, turned)
        other = jnp.where(row > col, both, turned)
        s_ref[q * T : (q + 1) * T, q * T : (q + 1) * T] = jnp.where(
            row == col, jnp.broadcast_to(diag_ref[n : n + 1, :], (T, T)), other
        )


def factor_kernel(g_ref, low_ref, high_ref, owner_row_ref, owner_ref, dest_ref, leaf_ref, piv_ref, pay_ref, s_ref, d_ref, inv_ref, diag_ref):
    for i in range(NT):
        for j in range(i):
            s_ref[i * T : (i + 1) * T, j * T : (j + 1) * T] = jnp.zeros((T, T), F32)
    leaf = leaf_ref[0]
    for parity in range(2):

        @pl.when(lax.rem(leaf, 2) == parity)
        def _():
            unpack(parity, g_ref, low_ref, high_ref, s_ref, diag_ref)

    split_pairs(s_ref, diag_ref)
    d_ref[...] = s_ref[:T, :T]

    def panel_step(p, _):
        diagonal_factor(d_ref, inv_ref)
        for q in range(NT):
            pl.when(p == q)(functools.partial(update_after, q, s_ref, d_ref, inv_ref))
        return 0

    lax.fori_loop(0, NT, panel_step, 0)
    piv_ref[0] = s_ref[pl.ds(pl.multiple_of(leaf * (PIV // NLEAF), 8), PIV // NLEAF), :]
    block = s_ref[pl.ds(pl.multiple_of(PIV + leaf * CB_DEV, 8), CB_DEV), PIV:]
    owner = owner_ref[...]
    same = owner == owner_row_ref[...]
    earlier = lax.broadcasted_iota(jnp.int32, (CB_DEV, CB_DEV), 1) < lax.broadcasted_iota(jnp.int32, (CB_DEV, CB_DEV), 0)
    slot = jnp.sum(jnp.where(same & earlier, 1.0, 0.0), axis=1, keepdims=True).astype(jnp.int32)
    place = slot * NFRONT + owner
    pick = (place == lax.broadcasted_iota(jnp.int32, (CB_DEV, CAP * NFRONT), 1)).astype(F32)
    marks = jnp.broadcast_to((dest_ref[...] + 1).astype(F32), (CB_DEV, T))
    send = lax.dot_general(
        pick, jnp.concatenate([block, marks], axis=1), (((0,), (0,)), ((), ())), precision=HIGHEST, preferred_element_type=F32
    )
    lane = lax.broadcasted_iota(jnp.int32, (NFRONT, T), 1)
    meta = jnp.zeros((NFRONT, T), F32)
    for k in range(CAP):
        part = send[k * NFRONT : (k + 1) * NFRONT, :]
        for t in range(CB // T):
            pay_ref[pl.ds(k * (CB // T) + t, NFRONT, stride=16), :] = part[:, t * T : (t + 1) * T]
        meta = jnp.where(lane == k, part[:, CB:], meta)
    pay_ref[pl.ds(15, NFRONT, stride=16), :] = meta


def factor(g, low, high, owner_row, owner, dest, leaf):
    vmem = pl.BlockSpec(memory_space=pltpu.VMEM)
    return pl.pallas_call(
        factor_kernel,
        out_shape=(
            jax.ShapeDtypeStruct((1, PIV // NLEAF, COLS), F32),
            jax.ShapeDtypeStruct((NFRONT * 16, T), F32),
        ),
        in_specs=[vmem] * 6 + [pl.BlockSpec(memory_space=pltpu.SMEM)],
        out_specs=(vmem, vmem),
        scratch_shapes=[pltpu.VMEM((COLS, COLS), F32), pltpu.VMEM((T, T), F32), pltpu.VMEM((T, T), F32), pltpu.VMEM((8, T), F32)],
        name="factor",
        compiler_params=pltpu.CompilerParams(vmem_limit_bytes=24 << 20),
    )(g, low, high, owner_row, owner, dest, leaf)


def assemble_kernel(pay_ref, out_ref):
    meta = pay_ref[pl.ds(15, NFRONT, stride=16), :]
    target = lax.broadcasted_iota(jnp.int32, (NFRONT, PR_DEV), 1).astype(F32) + 1.0
    total = jnp.zeros((PR_DEV, CB), F32)
    for k in range(CAP):
        hits = (meta[:, k : k + 1] == target).astype(F32)
        rows = jnp.concatenate(
            [pay_ref[pl.ds(k * (CB // T) + t, NFRONT, stride=16), :] for t in range(CB // T)], axis=1
        )
        total = total + lax.dot_general(
            hits, rows, (((0,), (0,)), ((), ())), precision=HIGHEST, preferred_element_type=F32
        )
    out_ref[0] = total


def assemble(pay):
    vmem = pl.BlockSpec(memory_space=pltpu.VMEM)
    return pl.pallas_call(
        assemble_kernel,
        out_shape=jax.ShapeDtypeStruct((1, PR_DEV, CB), F32),
        in_specs=[vmem],
        out_specs=vmem,
        name="assemble",
        compiler_params=pltpu.CompilerParams(vmem_limit_bytes=16 << 20),
    )(pay)


def shards(stacked, row_owner, dest_local):
    gram = local_gram(stacked)
    piece = lax.optimization_barrier(lax.psum_scatter(gram, "leaf", scatter_dimension=0, tiled=True))
    groups = [list(range(first, NLEAF, 2)) for first in range(2)]
    own = lax.all_gather(piece, "leaf", axis=0, axis_index_groups=groups)
    low = lax.ppermute(own[:HALF], "leaf", [(z, (z + 1) % NLEAF) for z in range(NLEAF)])
    high = lax.ppermute(own[HALF:], "leaf", [(z, (z - 1) % NLEAF) for z in range(NLEAF)])
    owner = row_owner[0]
    dest = dest_local.reshape(CB_DEV, 1)
    leaf = lax.axis_index("leaf").astype(jnp.int32).reshape(1)
    piv, pay = factor(own, low, high, owner.reshape(1, CB_DEV), owner, dest, leaf)
    got = lax.all_to_all(pay, "front", 0, 0, tiled=True)
    return piv, assemble(got)


def solution(mesh):
    return jax.shard_map(
        shards,
        mesh=mesh,
        in_specs=(P("front", "leaf", None), P("front", "leaf", None), P("front", "leaf")),
        out_specs=(P("front", "leaf", None), P("front", "leaf", None)),
        check_vma=False,
    )
```

```python
import functools
import jax
import jax.numpy as jnp
from jax import lax
from jax.experimental import pallas as pl
from jax.experimental.pallas import tpu as pltpu
from jax.sharding import PartitionSpec as P

PIV = 256
PR_DEV = 64
COLS = 896
CB = 640
CB_DEV = 40
CAP = 3
T = 128
NT = COLS // T
SUB = 8
NLEAF = 16
NFRONT = 32
PAIRS = ((0, 1), (2, 3), (4, 5))
LONE = NT - 1
TILES = NT * (NT + 1) // 2
FULL = (TILES - len(PAIRS)) * T
SHARD = 201
HALF = NLEAF // 4
F32 = jnp.float32
BF16 = jnp.bfloat16
HIGHEST = lax.Precision.HIGHEST


def tile_index(i, j):
    return i * NT - i * (i - 1) // 2 + (j - i)


def packed_tiles():
    order = [(i, j) for i in range(NT) for j in range(i + 1, NT)]
    return order + [(LONE, LONE)] + [(p, p) for p, _ in PAIRS]


def pieces(start, stop):
    while start < stop:
        chunk, rest = divmod(start, SHARD)
        size = min(stop - start, SHARD - rest)
        yield start, chunk, rest, size
        start += size


def square_iota(axis):
    return lax.broadcasted_iota(jnp.int32, (T, T), axis)


def halves(x):
    high = x.astype(BF16)
    return high, (x - high.astype(F32)).astype(BF16)


def dot_t(a, b):
    return lax.dot_general(a, b, (((0,), (0,)), ((), ())), preferred_element_type=F32)


def dot3_t(a, b):
    return dot_t(a[0], b[0]) + (dot_t(a[0], b[1]) + dot_t(a[1], b[0]))


def dot3(a, b):
    mm = functools.partial(jnp.dot, preferred_element_type=F32)
    return mm(a[0], b[0]) + (mm(a[0], b[1]) + mm(a[1], b[0]))


def gram_kernel(x_ref, out_ref, acc_ref):
    step = pl.program_id(0)

    @pl.when(step == 0)
    def _():
        acc_ref[...] = jnp.zeros_like(acc_ref)

    high, low = halves(x_ref[0])
    for start in range(0, COLS, 2 * T):
        stop = min(start + 2 * T, COLS)
        a = (high[:, :stop], low[:, :stop])
        b = (high[:, start:stop], low[:, start:stop])
        block = dot3_t(a, b)
        for j in range(start // T, stop // T):
            for i in range(j + 1):
                row = tile_index(i, j) * T
                acc_ref[row : row + T, :] += block[i * T : (i + 1) * T, j * T - start : (j + 1) * T - start]

    @pl.when(step == pl.num_programs(0) - 1)
    def _():
        def tile(i, j):
            row = tile_index(i, j) * T
            return acc_ref[row : row + T, :]

        row, col = square_iota(0), square_iota(1)
        partner = dict(PAIRS)
        for n, (i, j) in enumerate(packed_tiles()):
            value = tile(i, j)
            if i == j and i in partner:
                q = partner[i]
                other = tile(q, q)
                value = jnp.where(row <= col, value, other)
                at = FULL + PAIRS.index((i, q))
                out_ref[at : at + 1, :] = jnp.sum(jnp.where(row == col, other, 0.0), axis=0, keepdims=True)
            out_ref[n * T : (n + 1) * T, :] = value
        spare = FULL + len(PAIRS)
        out_ref[spare : NLEAF * SHARD, :] = jnp.zeros((NLEAF * SHARD - spare, T), F32)


def local_gram(stacked):
    rows = stacked.shape[1]
    chunk = 512
    return pl.pallas_call(
        gram_kernel,
        out_shape=jax.ShapeDtypeStruct((NLEAF * SHARD, T), F32),
        grid=(rows // chunk,),
        in_specs=[pl.BlockSpec((1, chunk, COLS), lambda k: (0, k, 0))],
        out_specs=pl.BlockSpec((NLEAF * SHARD, T), lambda k: (0, 0)),
        scratch_shapes=[pltpu.VMEM((TILES * T, T), F32)],
        name="local_gram",
        compiler_params=pltpu.CompilerParams(vmem_limit_bytes=61 << 20),
    )(stacked)


def lanes_of(x, lane):
    return jnp.take_along_axis(x, jnp.full((SUB, T), lane, jnp.int32), axis=1)


def row_of(x, row):
    return jnp.broadcast_to(x[row : row + 1, :], (SUB, T))


def diagonal_factor(d_ref, inv_ref):
    lane = lax.broadcasted_iota(jnp.int32, (SUB, T), 1)
    sub = lax.broadcasted_iota(jnp.int32, (SUB, T), 0)
    is_row = [sub == k for k in range(SUB)]
    nb = T // SUB
    rows = [d_ref[SUB * i : SUB * (i + 1), :] for i in range(nb)]
    start = list(rows)
    for b in range(nb):
        c0 = SUB * b
        inside = (lane >= c0) & (lane < c0 + SUB)
        col = [lanes_of(rows[b], c0 + k) for k in range(SUB)]
        work = jnp.where(inside, (lane == sub + c0).astype(F32), rows[b])
        done = jnp.zeros((SUB, T), F32)
        first = [row_of(lanes_of(start[b], c0 + k), k) for k in range(0, SUB, 2)]
        scale = [lax.rsqrt(v) for v in first]
        scale = [v * v for v in scale]
        pivot, cross, partner = row_of(col[0], 0), row_of(col[1], 0), row_of(col[1], 1)
        for k in range(0, SUB, 2):
            share = pivot * scale[k // 2]
            det = partner * share - cross * (cross * scale[k // 2])
            root_det = lax.rsqrt(det)
            root = lax.rsqrt(pivot)
            inverse = root * root
            second = root_det * root_det * share
            second_root = root_det * (share * lax.rsqrt(share))
            for q, (one, two) in ((k, (root, inverse)), (k + 1, (second_root, second))):
                ahead = [row_of(col[j], q) if j > q else None for j in range(SUB)]
                if q > k and q + 1 < SUB:
                    near, far = ahead[q + 1], ahead[q + 2]
                    pivot = row_of(col[q + 1], q + 1) - (near * near) * two
                    cross = row_of(col[q + 2], q + 1) - (near * far) * two
                    partner = row_of(col[q + 2], q + 2) - (far * far) * two
                for j in range(q + 1, SUB):
                    prod = col[q] * ahead[j]
                    col[j] = jnp.where(is_row[q], ahead[j] * two, col[j] - prod * two)
                rk = row_of(work, q)
                done = jnp.where(is_row[q], rk * one, done)
                pk = rk * two
                work = jnp.where(is_row[q], pk, work - col[q] * pk)
        inv_ref[c0 : c0 + SUB, :] = jnp.where(lane < c0 + SUB, done, 0.0)
        if b + 1 < nb:
            solved = [row_of(work, k) for k in range(SUB)]
        for i in range(b + 1, nb):
            terms = [lanes_of(rows[i], c0 + k) * solved[k] for k in range(SUB)]
            while len(terms) > 1:
                terms = [terms[q] + terms[q + 1] for q in range(0, len(terms), 2)]
            rows[i] = jnp.where(inside, 0.0, rows[i]) - terms[0]


def update_after(p, s_ref, d_ref, inv_ref):
    base = p * T
    after = base + T
    panel = dot3(halves(inv_ref[...]), halves(s_ref[base:after, base:]))
    upper = lax.broadcasted_iota(jnp.int32, (T, T), 1) >= lax.broadcasted_iota(jnp.int32, (T, T), 0)
    s_ref[base:after, base:after] = jnp.where(upper, panel[:, :T], 0.0)
    if after == COLS:
        return
    panel = panel[:, T:]
    s_ref[base:after, after:] = panel
    split = halves(panel)
    for i in range(p + 1, NT):
        lo = i * T - after
        left = tuple(v[:, lo : lo + T] for v in split)
        right = tuple(v[:, lo:] for v in split)
        block = s_ref[i * T : (i + 1) * T, i * T :] - dot3_t(left, right)
        s_ref[i * T : (i + 1) * T, i * T :] = block
        if i == p + 1:
            d_ref[...] = block[:, :T]


def unpack(parity, g_ref, low_ref, high_ref, s_ref, diag_ref):
    def move(dst, row, col, start, stop):
        for first, chunk, rest, size in pieces(start, stop):
            member = chunk // 2
            src = g_ref
            if chunk % 2 != parity:
                src, member = (low_ref, member) if member < HALF else (high_ref, member - HALF)
            to = row + first - start
            dst[to : to + size, col : col + T] = src[member, rest : rest + size, :]

    for n, (i, j) in enumerate(packed_tiles()):
        move(s_ref, i * T, j * T, n * T, (n + 1) * T)
    move(diag_ref, 0, 0, FULL, FULL + len(PAIRS))


def split_pairs(s_ref, diag_ref):
    row, col = square_iota(0), square_iota(1)
    for n, (p, q) in enumerate(PAIRS):
        both = s_ref[p * T : (p + 1) * T, p * T : (p + 1) * T]
        turned = jnp.transpose(both)
        s_ref[p * T : (p + 1) * T, p * T : (p + 1) * T] = jnp.where(row <= col, both, turned)
        other = jnp.where(row > col, both, turned)
        s_ref[q * T : (q + 1) * T, q * T : (q + 1) * T] = jnp.where(
            row == col, jnp.broadcast_to(diag_ref[n : n + 1, :], (T, T)), other
        )


def factor_kernel(g_ref, low_ref, high_ref, owner_row_ref, owner_ref, dest_ref, leaf_ref, piv_ref, pay_ref, s_ref, d_ref, inv_ref, diag_ref):
    for i in range(NT):
        for j in range(i):
            s_ref[i * T : (i + 1) * T, j * T : (j + 1) * T] = jnp.zeros((T, T), F32)
    leaf = leaf_ref[0]
    for parity in range(2):

        @pl.when(lax.rem(leaf, 2) == parity)
        def _():
            unpack(parity, g_ref, low_ref, high_ref, s_ref, diag_ref)

    split_pairs(s_ref, diag_ref)
    d_ref[...] = s_ref[:T, :T]

    def panel_step(p, _):
        diagonal_factor(d_ref, inv_ref)
        for q in range(NT):
            pl.when(p == q)(functools.partial(update_after, q, s_ref, d_ref, inv_ref))
        return 0

    lax.fori_loop(0, NT, panel_step, 0)
    piv_ref[0] = s_ref[pl.ds(pl.multiple_of(leaf * (PIV // NLEAF), 8), PIV // NLEAF), :]
    block = s_ref[pl.ds(pl.multiple_of(PIV + leaf * CB_DEV, 8), CB_DEV), PIV:]
    owner = owner_ref[...]
    same = owner == owner_row_ref[...]
    earlier = lax.broadcasted_iota(jnp.int32, (CB_DEV, CB_DEV), 1) < lax.broadcasted_iota(jnp.int32, (CB_DEV, CB_DEV), 0)
    slot = jnp.sum(jnp.where(same & earlier, 1.0, 0.0), axis=1, keepdims=True).astype(jnp.int32)
    place = slot * NFRONT + owner
    pick = (place == lax.broadcasted_iota(jnp.int32, (CB_DEV, CAP * NFRONT), 1)).astype(F32)
    marks = jnp.broadcast_to((dest_ref[...] + 1).astype(F32), (CB_DEV, T))
    send = lax.dot_general(
        pick, jnp.concatenate([block, marks], axis=1), (((0,), (0,)), ((), ())), precision=HIGHEST, preferred_element_type=F32
    )
    lane = lax.broadcasted_iota(jnp.int32, (NFRONT, T), 1)
    meta = jnp.zeros((NFRONT, T), F32)
    for k in range(CAP):
        part = send[k * NFRONT : (k + 1) * NFRONT, :]
        for t in range(CB // T):
            pay_ref[pl.ds(k * (CB // T) + t, NFRONT, stride=16), :] = part[:, t * T : (t + 1) * T]
        meta = jnp.where(lane == k, part[:, CB:], meta)
    pay_ref[pl.ds(15, NFRONT, stride=16), :] = meta


def factor(g, low, high, owner_row, owner, dest, leaf):
    vmem = pl.BlockSpec(memory_space=pltpu.VMEM)
    return pl.pallas_call(
        factor_kernel,
        out_shape=(
            jax.ShapeDtypeStruct((1, PIV // NLEAF, COLS), F32),
            jax.ShapeDtypeStruct((NFRONT * 16, T), F32),
        ),
        in_specs=[vmem] * 6 + [pl.BlockSpec(memory_space=pltpu.SMEM)],
        out_specs=(vmem, vmem),
        scratch_shapes=[pltpu.VMEM((COLS, COLS), F32), pltpu.VMEM((T, T), F32), pltpu.VMEM((T, T), F32), pltpu.VMEM((8, T), F32)],
        name="factor",
        compiler_params=pltpu.CompilerParams(vmem_limit_bytes=24 << 20),
    )(g, low, high, owner_row, owner, dest, leaf)


def assemble_kernel(pay_ref, out_ref):
    meta = pay_ref[pl.ds(15, NFRONT, stride=16), :]
    target = lax.broadcasted_iota(jnp.int32, (NFRONT, PR_DEV), 1).astype(F32) + 1.0
    total = jnp.zeros((PR_DEV, CB), F32)
    for k in range(CAP):
        hits = (meta[:, k : k + 1] == target).astype(F32)
        rows = jnp.concatenate(
            [pay_ref[pl.ds(k * (CB // T) + t, NFRONT, stride=16), :] for t in range(CB // T)], axis=1
        )
        total = total + lax.dot_general(
            hits, rows, (((0,), (0,)), ((), ())), precision=HIGHEST, preferred_element_type=F32
        )
    out_ref[0] = total


def assemble(pay):
    vmem = pl.BlockSpec(memory_space=pltpu.VMEM)
    return pl.pallas_call(
        assemble_kernel,
        out_shape=jax.ShapeDtypeStruct((1, PR_DEV, CB), F32),
        in_specs=[vmem],
        out_specs=vmem,
        name="assemble",
        compiler_params=pltpu.CompilerParams(vmem_limit_bytes=16 << 20),
    )(pay)


def shards(stacked, row_owner, dest_local):
    gram = local_gram(stacked)
    piece = lax.optimization_barrier(lax.psum_scatter(gram, "leaf", scatter_dimension=0, tiled=True))
    groups = [list(range(first, NLEAF, 2)) for first in range(2)]
    own = lax.all_gather(piece, "leaf", axis=0, axis_index_groups=groups)
    low = lax.ppermute(own[:HALF], "leaf", [(z, (z + 1) % NLEAF) for z in range(NLEAF)])
    high = lax.ppermute(own[HALF:], "leaf", [(z, (z - 1) % NLEAF) for z in range(NLEAF)])
    owner = row_owner[0]
    dest = dest_local.reshape(CB_DEV, 1)
    leaf = lax.axis_index("leaf").astype(jnp.int32).reshape(1)
    piv, pay = factor(own, low, high, owner.reshape(1, CB_DEV), owner, dest, leaf)
    got = lax.all_to_all(pay, "front", 0, 0, tiled=True)
    return piv, assemble(got)


def solution(mesh):
    return jax.shard_map(
        shards,
        mesh=mesh,
        in_specs=(P("front", "leaf", None), P("front", "leaf", None), P("front", "leaf")),
        out_specs=(P("front", "leaf", None), P("front", "leaf", None)),
        check_vma=False,
    )
```

```python
import functools
import jax
import jax.numpy as jnp
from jax import lax
from jax.experimental import pallas as pl
from jax.experimental.pallas import tpu as pltpu
from jax.sharding import PartitionSpec as P

PIV = 256
PR_DEV = 64
COLS = 896
CB = 640
CB_DEV = 40
CAP = 3
T = 128
NT = COLS // T
SUB = 8
NLEAF = 16
NFRONT = 32
PAIRS = ((0, 1), (2, 3), (4, 5))
LONE = NT - 1
TILES = NT * (NT + 1) // 2
FULL = (TILES - len(PAIRS)) * T
SHARD = 201
HALF = NLEAF // 4
F32 = jnp.float32
BF16 = jnp.bfloat16
HIGHEST = lax.Precision.HIGHEST


def tile_index(i, j):
    return i * NT - i * (i - 1) // 2 + (j - i)


def stacked_t(a, b):
    left = jnp.concatenate(a, axis=0)
    return dot_t(left, jnp.concatenate((b[0], b[0]), axis=0)) + dot_t(a[0], b[1])


def stacked(a, b):
    mm = functools.partial(jnp.dot, preferred_element_type=F32)
    return mm(jnp.concatenate(a, axis=1), jnp.concatenate((b[0], b[0]), axis=0)) + mm(a[0], b[1])


def packed_tiles():
    order = [(i, j) for i in range(NT) for j in range(i + 1, NT)]
    return order + [(LONE, LONE)] + [(p, p) for p, _ in PAIRS]


def pieces(start, stop):
    while start < stop:
        chunk, rest = divmod(start, SHARD)
        size = min(stop - start, SHARD - rest)
        yield start, chunk, rest, size
        start += size


def square_iota(axis):
    return lax.broadcasted_iota(jnp.int32, (T, T), axis)


def halves(x):
    high = x.astype(BF16)
    return high, (x - high.astype(F32)).astype(BF16)


def dot_t(a, b):
    return lax.dot_general(a, b, (((0,), (0,)), ((), ())), preferred_element_type=F32)


def dot3_t(a, b):
    return dot_t(a[0], b[0]) + (dot_t(a[0], b[1]) + dot_t(a[1], b[0]))


def dot3(a, b):
    mm = functools.partial(jnp.dot, preferred_element_type=F32)
    return mm(a[0], b[0]) + (mm(a[0], b[1]) + mm(a[1], b[0]))


def gram_kernel(x_ref, out_ref, acc_ref):
    step = pl.program_id(0)

    @pl.when(step == 0)
    def _():
        acc_ref[...] = jnp.zeros_like(acc_ref)

    high, low = halves(x_ref[0])
    for start in range(0, COLS, 2 * T):
        stop = min(start + 2 * T, COLS)
        a = (high[:, :stop], low[:, :stop])
        b = (high[:, start:stop], low[:, start:stop])
        block = dot3_t(a, b)
        for j in range(start // T, stop // T):
            for i in range(j + 1):
                row = tile_index(i, j) * T
                acc_ref[row : row + T, :] += block[i * T : (i + 1) * T, j * T - start : (j + 1) * T - start]

    @pl.when(step == pl.num_programs(0) - 1)
    def _():
        def tile(i, j):
            row = tile_index(i, j) * T
            return acc_ref[row : row + T, :]

        row, col = square_iota(0), square_iota(1)
        partner = dict(PAIRS)
        for n, (i, j) in enumerate(packed_tiles()):
            value = tile(i, j)
            if i == j and i in partner:
                q = partner[i]
                other = tile(q, q)
                value = jnp.where(row <= col, value, other)
                at = FULL + PAIRS.index((i, q))
                out_ref[at : at + 1, :] = jnp.sum(jnp.where(row == col, other, 0.0), axis=0, keepdims=True)
            out_ref[n * T : (n + 1) * T, :] = value
        spare = FULL + len(PAIRS)
        out_ref[spare : NLEAF * SHARD, :] = jnp.zeros((NLEAF * SHARD - spare, T), F32)


def local_gram(stacked):
    rows = stacked.shape[1]
    chunk = 512
    return pl.pallas_call(
        gram_kernel,
        out_shape=jax.ShapeDtypeStruct((NLEAF * SHARD, T), F32),
        grid=(rows // chunk,),
        in_specs=[pl.BlockSpec((1, chunk, COLS), lambda k: (0, k, 0))],
        out_specs=pl.BlockSpec((NLEAF * SHARD, T), lambda k: (0, 0)),
        scratch_shapes=[pltpu.VMEM((TILES * T, T), F32)],
        name="local_gram",
        compiler_params=pltpu.CompilerParams(vmem_limit_bytes=61 << 20),
    )(stacked)


def lanes_of(x, lane):
    return jnp.take_along_axis(x, jnp.full((SUB, T), lane, jnp.int32), axis=1)


def row_of(x, row):
    return jnp.broadcast_to(x[row : row + 1, :], (SUB, T))


def diagonal_factor(d_ref, inv_ref):
    lane = lax.broadcasted_iota(jnp.int32, (SUB, T), 1)
    sub = lax.broadcasted_iota(jnp.int32, (SUB, T), 0)
    is_row = [sub == k for k in range(SUB)]
    nb = T // SUB
    rows = [d_ref[SUB * i : SUB * (i + 1), :] for i in range(nb)]
    start = list(rows)
    for b in range(nb):
        c0 = SUB * b
        inside = (lane >= c0) & (lane < c0 + SUB)
        col = [lanes_of(rows[b], c0 + k) for k in range(SUB)]
        work = jnp.where(inside, (lane == sub + c0).astype(F32), rows[b])
        done = jnp.zeros((SUB, T), F32)
        first = [row_of(lanes_of(start[b], c0 + k), k) for k in range(0, SUB, 2)]
        scale = [lax.rsqrt(v) for v in first]
        scale = [v * v for v in scale]
        pivot, cross, partner = row_of(col[0], 0), row_of(col[1], 0), row_of(col[1], 1)
        for k in range(0, SUB, 2):
            share = pivot * scale[k // 2]
            det = partner * share - cross * (cross * scale[k // 2])
            root_det = lax.rsqrt(det)
            root = lax.rsqrt(pivot)
            inverse = root * root
            second = root_det * root_det * share
            second_root = root_det * (share * lax.rsqrt(share))
            for q, (one, two) in ((k, (root, inverse)), (k + 1, (second_root, second))):
                ahead = [row_of(col[j], q) if j > q else None for j in range(SUB)]
                if q > k and q + 1 < SUB:
                    near, far = ahead[q + 1], ahead[q + 2]
                    pivot = row_of(col[q + 1], q + 1) - (near * near) * two
                    cross = row_of(col[q + 2], q + 1) - (near * far) * two
                    partner = row_of(col[q + 2], q + 2) - (far * far) * two
                for j in range(q + 1, SUB):
                    prod = col[q] * ahead[j]
                    col[j] = jnp.where(is_row[q], ahead[j] * two, col[j] - prod * two)
                rk = row_of(work, q)
                done = jnp.where(is_row[q], rk * one, done)
                pk = rk * two
                work = jnp.where(is_row[q], pk, work - col[q] * pk)
        inv_ref[c0 : c0 + SUB, :] = jnp.where(lane < c0 + SUB, done, 0.0)
        if b + 1 < nb:
            solved = [row_of(work, k) for k in range(SUB)]
        for i in range(b + 1, nb):
            terms = [lanes_of(rows[i], c0 + k) * solved[k] for k in range(SUB)]
            while len(terms) > 1:
                terms = [terms[q] + terms[q + 1] for q in range(0, len(terms), 2)]
            rows[i] = jnp.where(inside, 0.0, rows[i]) - terms[0]


def update_after(p, s_ref, d_ref, inv_ref):
    base = p * T
    after = base + T
    panel = stacked(halves(inv_ref[...]), halves(s_ref[base:after, base:]))
    upper = lax.broadcasted_iota(jnp.int32, (T, T), 1) >= lax.broadcasted_iota(jnp.int32, (T, T), 0)
    s_ref[base:after, base:after] = jnp.where(upper, panel[:, :T], 0.0)
    if after == COLS:
        return
    panel = panel[:, T:]
    s_ref[base:after, after:] = panel
    split = halves(panel)
    for i in range(p + 1, NT):
        lo = i * T - after
        left = tuple(v[:, lo : lo + T] for v in split)
        right = tuple(v[:, lo:] for v in split)
        block = s_ref[i * T : (i + 1) * T, i * T :] - stacked_t(left, right)
        s_ref[i * T : (i + 1) * T, i * T :] = block
        if i == p + 1:
            d_ref[...] = block[:, :T]


def unpack(parity, g_ref, low_ref, high_ref, s_ref, diag_ref):
    def move(dst, row, col, start, stop):
        for first, chunk, rest, size in pieces(start, stop):
            member = chunk // 2
            src = g_ref
            if chunk % 2 != parity:
                src, member = (low_ref, member) if member < HALF else (high_ref, member - HALF)
            to = row + first - start
            dst[to : to + size, col : col + T] = src[member, rest : rest + size, :]

    for n, (i, j) in enumerate(packed_tiles()):
        move(s_ref, i * T, j * T, n * T, (n + 1) * T)
    move(diag_ref, 0, 0, FULL, FULL + len(PAIRS))


def split_pairs(s_ref, diag_ref):
    row, col = square_iota(0), square_iota(1)
    for n, (p, q) in enumerate(PAIRS):
        both = s_ref[p * T : (p + 1) * T, p * T : (p + 1) * T]
        turned = jnp.transpose(both)
        s_ref[p * T : (p + 1) * T, p * T : (p + 1) * T] = jnp.where(row <= col, both, turned)
        other = jnp.where(row > col, both, turned)
        s_ref[q * T : (q + 1) * T, q * T : (q + 1) * T] = jnp.where(
            row == col, jnp.broadcast_to(diag_ref[n : n + 1, :], (T, T)), other
        )


def factor_kernel(g_ref, low_ref, high_ref, owner_row_ref, owner_ref, dest_ref, leaf_ref, piv_ref, pay_ref, s_ref, d_ref, inv_ref, diag_ref):
    for i in range(NT):
        for j in range(i):
            s_ref[i * T : (i + 1) * T, j * T : (j + 1) * T] = jnp.zeros((T, T), F32)
    leaf = leaf_ref[0]
    for parity in range(2):

        @pl.when(lax.rem(leaf, 2) == parity)
        def _():
            unpack(parity, g_ref, low_ref, high_ref, s_ref, diag_ref)

    split_pairs(s_ref, diag_ref)
    d_ref[...] = s_ref[:T, :T]

    def panel_step(p, _):
        diagonal_factor(d_ref, inv_ref)
        for q in range(NT):
            pl.when(p == q)(functools.partial(update_after, q, s_ref, d_ref, inv_ref))
        return 0

    lax.fori_loop(0, NT, panel_step, 0)
    piv_ref[0] = s_ref[pl.ds(pl.multiple_of(leaf * (PIV // NLEAF), 8), PIV // NLEAF), :]
    block = s_ref[pl.ds(pl.multiple_of(PIV + leaf * CB_DEV, 8), CB_DEV), PIV:]
    owner = owner_ref[...]
    same = owner == owner_row_ref[...]
    earlier = lax.broadcasted_iota(jnp.int32, (CB_DEV, CB_DEV), 1) < lax.broadcasted_iota(jnp.int32, (CB_DEV, CB_DEV), 0)
    slot = jnp.sum(jnp.where(same & earlier, 1.0, 0.0), axis=1, keepdims=True).astype(jnp.int32)
    place = slot * NFRONT + owner
    pick = (place == lax.broadcasted_iota(jnp.int32, (CB_DEV, CAP * NFRONT), 1)).astype(F32)
    marks = jnp.broadcast_to((dest_ref[...] + 1).astype(F32), (CB_DEV, T))
    send = lax.dot_general(
        pick, jnp.concatenate([block, marks], axis=1), (((0,), (0,)), ((), ())), precision=HIGHEST, preferred_element_type=F32
    )
    lane = lax.broadcasted_iota(jnp.int32, (NFRONT, T), 1)
    meta = jnp.zeros((NFRONT, T), F32)
    for k in range(CAP):
        part = send[k * NFRONT : (k + 1) * NFRONT, :]
        for t in range(CB // T):
            pay_ref[pl.ds(k * (CB // T) + t, NFRONT, stride=16), :] = part[:, t * T : (t + 1) * T]
        meta = jnp.where(lane == k, part[:, CB:], meta)
    pay_ref[pl.ds(15, NFRONT, stride=16), :] = meta


def factor(g, low, high, owner_row, owner, dest, leaf):
    vmem = pl.BlockSpec(memory_space=pltpu.VMEM)
    return pl.pallas_call(
        factor_kernel,
        out_shape=(
            jax.ShapeDtypeStruct((1, PIV // NLEAF, COLS), F32),
            jax.ShapeDtypeStruct((NFRONT * 16, T), F32),
        ),
        in_specs=[vmem] * 6 + [pl.BlockSpec(memory_space=pltpu.SMEM)],
        out_specs=(vmem, vmem),
        scratch_shapes=[pltpu.VMEM((COLS, COLS), F32), pltpu.VMEM((T, T), F32), pltpu.VMEM((T, T), F32), pltpu.VMEM((8, T), F32)],
        name="factor",
        compiler_params=pltpu.CompilerParams(vmem_limit_bytes=24 << 20),
    )(g, low, high, owner_row, owner, dest, leaf)


def assemble_kernel(pay_ref, out_ref):
    meta = pay_ref[pl.ds(15, NFRONT, stride=16), :]
    target = lax.broadcasted_iota(jnp.int32, (NFRONT, PR_DEV), 1).astype(F32) + 1.0
    total = jnp.zeros((PR_DEV, CB), F32)
    for k in range(CAP):
        hits = (meta[:, k : k + 1] == target).astype(F32)
        rows = jnp.concatenate(
            [pay_ref[pl.ds(k * (CB // T) + t, NFRONT, stride=16), :] for t in range(CB // T)], axis=1
        )
        total = total + lax.dot_general(
            hits, rows, (((0,), (0,)), ((), ())), precision=HIGHEST, preferred_element_type=F32
        )
    out_ref[0] = total


def assemble(pay):
    vmem = pl.BlockSpec(memory_space=pltpu.VMEM)
    return pl.pallas_call(
        assemble_kernel,
        out_shape=jax.ShapeDtypeStruct((1, PR_DEV, CB), F32),
        in_specs=[vmem],
        out_specs=vmem,
        name="assemble",
        compiler_params=pltpu.CompilerParams(vmem_limit_bytes=16 << 20),
    )(pay)


def shards(stacked, row_owner, dest_local):
    gram = local_gram(stacked)
    piece = lax.optimization_barrier(lax.psum_scatter(gram, "leaf", scatter_dimension=0, tiled=True))
    groups = [list(range(first, NLEAF, 2)) for first in range(2)]
    own = lax.all_gather(piece, "leaf", axis=0, axis_index_groups=groups)
    low = lax.ppermute(own[:HALF], "leaf", [(z, (z + 1) % NLEAF) for z in range(NLEAF)])
    high = lax.ppermute(own[HALF:], "leaf", [(z, (z - 1) % NLEAF) for z in range(NLEAF)])
    owner = row_owner[0]
    dest = dest_local.reshape(CB_DEV, 1)
    leaf = lax.axis_index("leaf").astype(jnp.int32).reshape(1)
    piv, pay = factor(own, low, high, owner.reshape(1, CB_DEV), owner, dest, leaf)
    got = lax.all_to_all(pay, "front", 0, 0, tiled=True)
    return piv, assemble(got)


def solution(mesh):
    return jax.shard_map(
        shards,
        mesh=mesh,
        in_specs=(P("front", "leaf", None), P("front", "leaf", None), P("front", "leaf")),
        out_specs=(P("front", "leaf", None), P("front", "leaf", None)),
        check_vma=False,
    )
```
